32 devices in a mesh: pipe: 4 (over y, x), expert: 8 (over z, core).
Axes of the slice: x: 2, y: 2, z: 4, core: 2. Of those that a mesh axis runs over, the one named last changes fastest.
Arguments:
- acts_a: bfloat16 [4, 512, 7168], P('pipe', 'expert'), may hold values from -6 to 6
- acts_b: bfloat16 [4, 512, 7168], P('pipe', 'expert'), may hold values from -6 to 6
- cot_b: bfloat16 [4, 512, 7168], P('pipe', 'expert'), may hold values from -1.5 to 1.5
- routes_a: int32 [4, 512, 2], P('pipe', 'expert'), may hold values from 0 to 3, all different within a row; in each aligned block of 64 rows (0 to 63, 64 to 127, ..., all dimensions but the last counted through in order) at most 34 rows name the same one
- gates_a: float32 [4, 512, 2], P('pipe', 'expert'), may hold values from 0.1 to 1
- routes_b: int32 [4, 512, 2], P('pipe', 'expert'), may hold values from 0 to 3, all different within a row; in each aligned block of 64 rows (0 to 63, 64 to 127, ..., all dimensions but the last counted through in order) at most 34 rows name the same one
- gates_b: float32 [4, 512, 2], P('pipe', 'expert'), may hold values from 0.1 to 1
- up_weight: bfloat16 [4, 28672, 1024], P('pipe', 'expert'), may hold values from -0.0625 to 0.0625
- down_weight: bfloat16 [4, 1024, 28672], P('pipe', None, 'expert'), may hold values from -0.1875 to 0.1875
- up_scale: float32 [4, 4], P('pipe'), may hold values from 0.002362278 to 0.004724556
- down_scale: float32 [4, 4], P('pipe'), may hold values from 0.00625 to 0.0125
Outputs:
- next_a: bfloat16 [4, 512, 7168], P('pipe', 'expert')
- next_cot_b: bfloat16 [4, 512, 7168], P('pipe', 'expert')
- up_grad: bfloat16 [4, 28672, 1024], P('pipe', 'expert')
- down_grad: bfloat16 [4, 1024, 28672], P('pipe', None, 'expert')
- up_scale_grad: float32 [4, 4], P('pipe')
- down_scale_grad: float32 [4, 4], P('pipe')
The draws below stay inside these ranges and needn't reach their ends.
Inputs may be any that keep to these rules, and one draw needn't show every extreme that they name: `routes_a`: within the rows of one device no expert is chosen by more than 34 rows, and some expert is chosen by exactly 34 rows there. `routes_b`: within the rows of one device no expert is chosen by more than 34 rows, and some expert is chosen by exactly 34 rows there.
All inputs are finite; a program needn't handle non-finite values.
Results may differ from the reference program's by a relative error of at most 0.0091.
Values may be sent and summed in bfloat16 or wider, within the bound.
No kernel may reach another device: no remote copies, remote signals or barrier semaphores. Data moves between devices by JAX's collectives and lax.ppermute only.
A program may use at most 128 MiB of HBM per device.

```python
import math
import jax
import jax.numpy as jnp
import numpy as np
from jax import lax

D = 7168
HID = 1024
EXPERTS = 4
TOP = 2
TOK_DEV = 64
TOKENS = 512
CAP = 34
N_PIPE = 4
N_EXPERT = 8


def level_of(own_key, extent, split, smallest, top_value):
    gain = 1.0
    for dim, parts in split:
        heights = jax.random.uniform(jax.random.fold_in(jax.random.fold_in(own_key, 6), dim), (parts,), jnp.float32, smallest / len(split), top_value / len(split))
        gain = gain * jnp.repeat(jnp.exp(heights), extent[dim] // parts).reshape((-1,) + (1,) * (len(extent) - 1 - dim))
    return gain


def assign_block(own_key, own, number, rows, count, top, most, lean):
    order = jax.random.permutation(own_key, count)
    crowded, common = load_shares(count, rows * top, most, lean, True), load_shares(count, rows * top, most, lean, False)
    places = jnp.arange(count)

    def named(lengths, offset_by):
        used = int((lengths > 0).sum())
        fixed = max(1, used // 4)
        passed = fixed + (places - fixed + offset_by * (used - fixed)) % max(1, count - fixed)
        return jnp.zeros((count,), jnp.int32).at[order[jnp.where(places < fixed, places, passed)]].set(jnp.asarray(lengths, jnp.int32))

    lengths = jnp.where(number % 4 == 0, named(crowded, number // 4), named(common, number - number // 4 - 1))
    mixed = jax.random.permutation(jax.random.fold_in(own, 3), count)
    donor, sink = mixed[0:count // 2 * 2:2], mixed[1:count // 2 * 2:2]
    room = jnp.minimum(lengths[donor] - 1, most - lengths[sink]) // 2
    room = jnp.where((donor == order[0]) | (sink == order[0]) | (lengths[sink] == 0), 0, jnp.maximum(room, 0))
    passed = jax.random.randint(jax.random.fold_in(own, 4), (count // 2,), 0, 1 << 20) % (room + 1)
    lengths = lengths.at[donor].add(-passed).at[sink].add(passed)
    members = jnp.searchsorted(jnp.cumsum(lengths), jnp.arange(rows * top), side="right").astype(jnp.int32)
    table = members.reshape(top, rows).T
    table = table[jax.random.permutation(jax.random.fold_in(own, 1), rows)]
    offset_by = jax.random.randint(jax.random.fold_in(own, 2), (rows, 1), 0, top)
    return jnp.take_along_axis(table, (jnp.arange(top)[None, :] + offset_by) % top, axis=1)


def load_shares(amount, total, limit, skew, full):
    weights = [(1 << 20) // math.isqrt(standing ** skew) + 1 for standing in range(1, amount + 1)]
    largest = limit if full else min(limit, max(-(-total // amount), total * weights[0] // sum(weights)))
    least = 1 if total - largest >= amount - 1 else 0
    given, rest = [largest] + [least] * (amount - 1), total - largest - least * (amount - 1)
    while rest > 0:
        free = [i for i in range(1, amount) if given[i] < largest] or [i for i in range(1, amount) if given[i] < limit]
        pool, remaining = sum([weights[i] for i in free]), rest
        for i in free:
            addition = min(limit - given[i], max(1, remaining * weights[i] // pool), rest)
            given[i] = given[i] + addition
            rest = rest - addition
    return np.array(given)


def noise(stream_key, extent, deviation, reach, cuts=(), held_as=jnp.bfloat16):
    values = jax.random.normal(stream_key, extent, jnp.float32) * deviation
    if len(cuts) > 0:
        values = level_of(stream_key, extent, cuts, -0.22, 0.18) * values
    return jnp.clip(values, min=-reach, max=reach).astype(held_as)


def setup_inputs(seed: int = 0) -> dict:
    arg_keys = jax.random.split(jax.random.key(seed), 12)
    acts_a = noise(arg_keys[0], (N_PIPE, TOKENS, D), 1.0, 6.0, ((0, 4), (1, 8)))
    acts_b = noise(arg_keys[1], (N_PIPE, TOKENS, D), 1.0, 6.0, ((0, 4), (1, 8)))
    cot_b = noise(arg_keys[2], (N_PIPE, TOKENS, D), 0.25, 1.5, ((0, 4), (1, 8)))
    routes_a_keys = jax.random.split(jax.random.fold_in(arg_keys[3], 1), N_PIPE * TOKENS // TOK_DEV)
    routes_a_turns = jax.random.permutation(jax.random.fold_in(arg_keys[3], 3), N_PIPE * TOKENS // TOK_DEV)
    routes_a = jax.vmap(lambda own, number: assign_block(jax.random.fold_in(arg_keys[3], 2), own, number, TOK_DEV, EXPERTS, TOP, CAP, 2))(routes_a_keys, routes_a_turns).reshape((N_PIPE, TOKENS, TOP))
    gates_a = jnp.clip(0.1 + 0.9 * jax.random.uniform(arg_keys[4], (N_PIPE, TOKENS, TOP), jnp.float32) ** level_of(arg_keys[4], (N_PIPE, TOKENS, TOP), ((0, 4), (1, 8)), -0.2, 0.2), 0.1, 1.0)
    routes_b_keys = jax.random.split(jax.random.fold_in(arg_keys[5], 1), N_PIPE * TOKENS // TOK_DEV)
    routes_b_turns = jax.random.permutation(jax.random.fold_in(arg_keys[5], 3), N_PIPE * TOKENS // TOK_DEV)
    routes_b = jax.vmap(lambda own, number: assign_block(jax.random.fold_in(arg_keys[5], 2), own, number, TOK_DEV, EXPERTS, TOP, CAP, 2))(routes_b_keys, routes_b_turns).reshape((N_PIPE, TOKENS, TOP))
    gates_b = jnp.clip(0.1 + 0.9 * jax.random.uniform(arg_keys[6], (N_PIPE, TOKENS, TOP), jnp.float32) ** level_of(arg_keys[6], (N_PIPE, TOKENS, TOP), ((0, 4), (1, 8)), -0.2, 0.2), 0.1, 1.0)
    up_weight = noise(arg_keys[7], (N_PIPE, EXPERTS * D, HID), D ** -0.5, 0.0625, ((0, 4), (1, 8)))
    down_weight = noise(arg_keys[8], (N_PIPE, HID, EXPERTS * D), HID ** -0.5, 0.1875, ((0, 4), (2, 8)))
    up_scale = jnp.clip(jnp.exp(math.log(0.004724556) - 0.6931472 * jax.random.uniform(arg_keys[9], (N_PIPE, EXPERTS), jnp.float32) ** level_of(arg_keys[9], (N_PIPE, EXPERTS), ((0, 4),), -0.2, 0.2)), 0.002362278, 0.004724556)
    down_scale = jnp.clip(jnp.exp(math.log(0.0125) - 0.6931472 * jax.random.uniform(arg_keys[10], (N_PIPE, EXPERTS), jnp.float32) ** level_of(arg_keys[10], (N_PIPE, EXPERTS), ((0, 4),), -0.2, 0.2)), 0.00625, 0.0125)
    return dict(acts_a=acts_a, acts_b=acts_b, cot_b=cot_b, routes_a=routes_a, gates_a=gates_a, routes_b=routes_b, gates_b=gates_b, up_weight=up_weight, down_weight=down_weight, up_scale=up_scale, down_scale=down_scale)


qlimit = 7.0
epsilon = 1e-06
two_pi = 2.0 * math.pi
highest = lax.Precision.HIGHEST

def rms_norm(values):
    return values * lax.rsqrt(lax.optimization_barrier(jnp.mean(values * values, axis=-1, keepdims=True)) + epsilon)

def soft_round(values):
    return values - jnp.sin(two_pi * values) / two_pi

def fake_quant(weights, scale):
    ratio = weights.astype(jnp.float32) / scale
    return scale * soft_round(jnp.clip(ratio, -qlimit, qlimit))

def quant_grads(weights, scale, grads):
    ratio = weights.astype(jnp.float32) / scale
    inside = jnp.abs(ratio) < qlimit
    wave = 1.0 - jnp.cos(two_pi * ratio)
    grads_wide = grads.astype(jnp.float32)
    weight_grad = grads_wide * jnp.where(inside, wave, 0.0)
    slope = soft_round(jnp.clip(ratio, -qlimit, qlimit)) - jnp.where(inside, ratio * wave, 0.0)
    scale_grad = lax.optimization_barrier(jnp.sum(grads_wide * slope, axis=(1, 2))) / math.sqrt(D * HID * qlimit)
    return (weight_grad, scale_grad)

def silu_grad(values):
    sigma_v = jax.nn.sigmoid(values)
    return sigma_v * (1.0 + values * (1.0 - sigma_v))

def route_tables(routes, gates):
    flat_ids = routes.reshape(-1)
    entries = flat_ids.shape[0]
    chosen = routes.shape[1]
    matches = (flat_ids[:, None] == jnp.arange(EXPERTS, dtype=jnp.int32)[None, :]).astype(jnp.int32)
    before = jnp.cumsum(matches, axis=0) - matches
    slot_of = lax.optimization_barrier(jnp.sum(before * matches, axis=1))
    at_slot = (slot_of[:, None] == jnp.arange(CAP, dtype=jnp.int32)[None, :]).astype(jnp.float32)
    owner_of = ((jnp.arange(entries, dtype=jnp.int32) // chosen)[:, None] == jnp.arange(routes.shape[0], dtype=jnp.int32)[None, :]).astype(jnp.float32)
    matches_wide = matches.astype(jnp.float32)
    dispatch = jnp.einsum('re,rc,rt->ect', matches_wide, at_slot, owner_of, precision=highest)
    weighted = jnp.einsum('re,rc,rt->ect', matches_wide * gates.reshape(-1)[:, None].astype(jnp.float32), at_slot, owner_of, precision=highest)
    return (dispatch, weighted)

def gather_rows(values, table):
    packed = jnp.einsum('nect,ntd->encd', table, values.astype(jnp.float32), precision=highest)
    return packed.astype(jnp.bfloat16).reshape(EXPERTS, N_EXPERT * CAP, D)

def scatter_rows(rows, table):
    shaped = rows.astype(jnp.float32).reshape(EXPERTS, N_EXPERT, CAP, D)
    return jnp.einsum('nect,encd->ntd', table, shaped, precision=highest)

def reference(acts_a, acts_b, cot_b, routes_a, gates_a, routes_b, gates_b, up_weight, down_weight, up_scale, down_scale):
    tables = jax.vmap(route_tables)
    empty = jnp.zeros((TOKENS, D), jnp.bfloat16)
    forward_out = [empty]
    backward_out = [empty for index in range(N_PIPE)]
    up_grads, down_grads, up_sgrads, down_sgrads = ([], [], [], [])
    for section in range(N_PIPE):
        up_blocks = up_weight[section].reshape(EXPERTS, D, HID)
        down_blocks = down_weight[section].reshape(HID, EXPERTS, D).transpose(1, 0, 2)
        up_steps = up_scale[section][:, None, None]
        down_steps = down_scale[section][:, None, None]
        q_up = fake_quant(up_blocks, up_steps).astype(jnp.bfloat16).astype(jnp.float32)
        q_down = fake_quant(down_blocks, down_steps).astype(jnp.bfloat16).astype(jnp.float32)
        x_a = acts_a[section].astype(jnp.float32).reshape(N_EXPERT, TOK_DEV, D)
        normed_a = rms_norm(x_a).astype(jnp.bfloat16)
        disp_a, comb_a = tables(routes_a[section].reshape(N_EXPERT, TOK_DEV, TOP), gates_a[section].reshape(N_EXPERT, TOK_DEV, TOP))
        rows_a = gather_rows(normed_a, disp_a).astype(jnp.float32)
        pre_a = jnp.einsum('erd,edh->erh', rows_a, q_up).astype(jnp.bfloat16)
        hidden_a = jax.nn.silu(pre_a.astype(jnp.float32)).astype(jnp.bfloat16)
        expert_a = jnp.einsum('erh,ehd->erd', hidden_a.astype(jnp.float32), q_down).astype(jnp.bfloat16)
        mixed = (x_a + scatter_rows(expert_a, comb_a)).astype(jnp.bfloat16).reshape(TOKENS, D)
        if section + 1 < N_PIPE:
            forward_out.append(mixed)
        x_b = acts_b[section].astype(jnp.float32).reshape(N_EXPERT, TOK_DEV, D)
        cot_here = cot_b[section].astype(jnp.float32).reshape(N_EXPERT, TOK_DEV, D)
        normed_wide, norm_back = jax.vjp(rms_norm, x_b)
        disp_b, comb_b = tables(routes_b[section].reshape(N_EXPERT, TOK_DEV, TOP), gates_b[section].reshape(N_EXPERT, TOK_DEV, TOP))
        rows_b = gather_rows(normed_wide.astype(jnp.bfloat16), disp_b).astype(jnp.float32)
        cots_b = gather_rows(cot_here, comb_b).astype(jnp.float32)
        pre_b = jnp.einsum('erd,edh->erh', rows_b, q_up).astype(jnp.bfloat16).astype(jnp.float32)
        hidden_b = jax.nn.silu(pre_b).astype(jnp.bfloat16).astype(jnp.float32)
        hidden_grad = jnp.einsum('erd,ehd->erh', cots_b, q_down).astype(jnp.bfloat16).astype(jnp.float32)
        pre_grad = (hidden_grad * silu_grad(pre_b)).astype(jnp.bfloat16).astype(jnp.float32)
        input_rows = jnp.einsum('erh,edh->erd', pre_grad, q_up).astype(jnp.bfloat16)
        up_gq = jnp.einsum('erd,erh->edh', rows_b, pre_grad).astype(jnp.bfloat16)
        down_gq = jnp.einsum('erh,erd->ehd', hidden_b, cots_b).astype(jnp.bfloat16)
        back_b, = norm_back(scatter_rows(input_rows, disp_b))
        grad_in = (cot_here + back_b).astype(jnp.bfloat16).reshape(TOKENS, D)
        if section > 0:
            backward_out[section - 1] = grad_in
        up_w, up_s = quant_grads(up_blocks, up_steps, up_gq)
        down_w, down_s = quant_grads(down_blocks, down_steps, down_gq)
        up_grads.append(up_w.reshape(EXPERTS * D, HID).astype(jnp.bfloat16))
        down_grads.append(down_w.transpose(1, 0, 2).reshape(HID, EXPERTS * D).astype(jnp.bfloat16))
        up_sgrads.append(up_s)
        down_sgrads.append(down_s)
    return (jnp.stack(forward_out), jnp.stack(backward_out), jnp.stack(up_grads), jnp.stack(down_grads), jnp.stack(up_sgrads), jnp.stack(down_sgrads))
```

```python
import math

import jax
import jax.numpy as jnp
from jax import lax
from jax.sharding import PartitionSpec as P

EXPERTS = 4
CAP = 34


qlimit = 7.0
epsilon = 1e-06

F_POLY = (3.99999827, -10.31875998, 10.67036777, -6.06749521, 1.94699036)
W_POLY = (19.73920584, -64.93916223, 85.45076959, -60.17190643, 25.98146098, -6.54589238)


def horner(coefs, z):
    acc = jnp.full_like(z, coefs[-1])
    for c in coefs[-2::-1]:
        acc = acc * z + c
    return acc


def reduced(weights, inv_scale):
    u = jnp.clip(weights.astype(jnp.float32) * inv_scale, -qlimit, qlimit)
    return u, u - jnp.round(u)


def fake_quant(weights, scale, inv_scale):
    u, r = reduced(weights, inv_scale)
    z = r * r
    return (scale * (u - r * ((0.25 - z) * horner(F_POLY, z)))).astype(jnp.bfloat16)


def quant_grads(weights, inv_scale, grads):
    u, r = reduced(weights, inv_scale)
    z = r * r
    weight_grad = grads * (z * horner(W_POLY, z))
    return weight_grad.astype(jnp.bfloat16), jnp.sum(weight_grad * u)


def dot(a, b, dims=(((1,), (0,)), ((), ()))):
    return lax.dot_general(a, b, dims, preferred_element_type=jnp.float32)


def rounded(value):
    return lax.reduce_precision(value, exponent_bits=8, mantissa_bits=7)


LAST = (((1,), (1,)), ((), ()))
FIRST = (((0,), (0,)), ((), ()))


def shards(
    acts_a,
    acts_b,
    cot_b,
    routes_a,
    gates_a,
    routes_b,
    gates_b,
    up_weight,
    down_weight,
    up_scale,
    down_scale,
):
    peers = lax.axis_size("expert")
    stages = lax.axis_size("pipe")
    parts = peers // EXPERTS
    device_id = lax.axis_index("expert")
    expert_id = device_id // parts
    part_id = device_id % parts
    tokens, width = acts_a.shape[1], acts_a.shape[2]
    part_width = width // parts

    def swap(value, distance):
        return lax.ppermute(value, "expert", [(i, i ^ distance) for i in range(peers)])

    def part_sum(value):
        distance = 1
        while distance < parts:
            value = value + swap(value, distance)
            distance *= 2
        return value

    def token_sum(value):
        distance = 1
        while distance < parts:
            other = jnp.split(swap(value, distance), parts, axis=0)
            value = value + jnp.concatenate([other[k ^ distance] for k in range(parts)], axis=0)
            distance *= 2
        return value

    def spread(value):
        pieces = []
        for k in range(parts):
            start = (part_id ^ k) * part_width
            piece = lax.dynamic_slice_in_dim(value, start, part_width, axis=1)
            pieces.append(swap(piece, k) if k else piece)
        return jnp.concatenate(pieces, axis=0)

    def share(value):
        pieces = [swap(value, k) if k else value for k in range(parts)]
        return jnp.concatenate(pieces, axis=0)

    def exchange(blocks):
        return [swap(b, k * parts) if k else b for k, b in enumerate(blocks)]

    def pass_on(value, by):
        pieces = []
        for k in range(parts):
            block = value[k * tokens : (k + 1) * tokens]
            pairs = [
                (s * peers + i, (s + by) * peers + (i ^ k))
                for s in range(stages)
                if 0 <= s + by < stages
                for i in range(peers)
            ]
            pieces.append(lax.ppermute(block, ("pipe", "expert"), pairs))
        columns = []
        for q in range(parts):
            column = pieces[0]
            for k in range(1, parts):
                column = jnp.where((part_id ^ k) == q, pieces[k], column)
            columns.append(column)
        return jnp.concatenate(columns, axis=1)

    def one_hots(routes):
        near = jnp.bitwise_xor(routes, expert_id)
        matches = (near[:, :, None] == jnp.arange(EXPERTS)).astype(jnp.float32)
        both = matches.sum(1)
        lower = (jnp.arange(tokens)[:, None] > jnp.arange(tokens)[None, :]).astype(jnp.float32)
        earlier = dot(lower, both)
        chosen, seen = [], earlier
        for j in range(routes.shape[1]):
            m = matches[:, j]
            slot = jnp.sum(m * seen, axis=1)
            at_slot = (slot[:, None] == jnp.arange(CAP, dtype=jnp.float32)).astype(jnp.float32)
            chosen.append(m[:, :, None] * at_slot[:, None, :])
            seen = seen + m
        return chosen

    def group_hots(routes):
        hots = []
        for block in range(parts):
            hots.append(one_hots(routes[block * tokens : (block + 1) * tokens]))
        out = []
        for j in range(routes.shape[1]):
            rows = []
            for block in range(parts):
                here = (jnp.arange(parts) == (part_id ^ block)).astype(jnp.float32)
                rows.append(hots[block][j][:, :, None, :] * here[None, None, :, None])
            out.append(jnp.concatenate(rows, axis=0).reshape(parts * tokens, -1))
        return out

    def pack(hot, values):
        return dot(hot, values, FIRST)

    def split(rows):
        return jnp.split(rows, EXPERTS, axis=0)

    is_mine = (jnp.arange(EXPERTS, dtype=jnp.int32) == expert_id).astype(jnp.float32)
    s_up = jnp.sum(is_mine * up_scale[0])
    s_down = jnp.sum(is_mine * down_scale[0])
    inv_up, inv_down = 1.0 / s_up, 1.0 / s_down
    w_up, w_down = up_weight[0], down_weight[0]

    def inv_rms(x):
        wide = x.astype(jnp.float32)
        return lax.rsqrt(jnp.mean(wide * wide, axis=-1, keepdims=True) + epsilon)

    small = jnp.concatenate(
        [
            routes_b[0].astype(jnp.float32),
            gates_b[0],
            inv_rms(acts_b[0]),
            routes_a[0].astype(jnp.float32),
            gates_a[0],
            inv_rms(acts_a[0]),
        ],
        axis=1,
    )
    small = share(small)
    top = routes_a.shape[2]
    routes_gb, gates_gb, rms_b, routes_ga, gates_ga, rms_a = jnp.split(
        small, [top, 2 * top, 2 * top + 1, 3 * top + 1, 4 * top + 1], axis=1
    )
    x_b, c_b, x_a = spread(acts_b[0]), spread(cot_b[0]), spread(acts_a[0])

    hots_b = group_hots(routes_gb.astype(jnp.int32))
    hot_b = sum(hots_b).astype(jnp.bfloat16)
    gate_b = sum(jnp.sum(h * gates_gb[:, j : j + 1], axis=0) for j, h in enumerate(hots_b))
    norm_b = (x_b.astype(jnp.float32) * rms_b).astype(jnp.bfloat16)
    rows_u = jnp.concatenate(exchange(split(pack(hot_b, norm_b).astype(jnp.bfloat16))), axis=0)
    send_c = (pack(hot_b, c_b) * gate_b[:, None]).astype(jnp.bfloat16)
    rows_c = jnp.concatenate(exchange(split(send_c)), axis=0)

    hots_a = [h.astype(jnp.bfloat16) for h in group_hots(routes_ga.astype(jnp.int32))]
    norm_a = (x_a.astype(jnp.float32) * rms_a).astype(jnp.bfloat16)
    rows_a = jnp.concatenate(exchange(split(pack(sum(hots_a), norm_a).astype(jnp.bfloat16))), axis=0)

    q_up, q_down = lax.optimization_barrier(
        (fake_quant(w_up, s_up, inv_up), fake_quant(w_down, s_down, inv_down))
    )

    own_pre_b = dot(rows_u, q_up)
    pre_b = rounded(part_sum(own_pre_b))
    own_grad = dot(rows_c, q_down, LAST)
    hidden_grad = rounded(part_sum(own_grad))
    sigma = jax.nn.sigmoid(pre_b)
    hidden_b = (pre_b * sigma).astype(jnp.bfloat16)
    pre_grad = (hidden_grad * sigma * (1.0 + pre_b * (1.0 - sigma))).astype(jnp.bfloat16)
    input_rows = dot(pre_grad, q_up, LAST).astype(jnp.bfloat16)
    back = jnp.concatenate(exchange(split(input_rows)), axis=0)

    dw_up, sum_up = quant_grads(w_up, inv_up, dot(rows_u, pre_grad, FIRST))
    dw_down, sum_down = quant_grads(w_down, inv_down, dot(hidden_b, rows_c, FIRST))
    quant_up = jnp.sum(pre_grad.astype(jnp.float32) * own_pre_b)
    quant_down = jnp.sum(hidden_b.astype(jnp.float32) * own_grad)
    root = math.sqrt(w_up.size * parts * qlimit)
    ds_up = (quant_up * inv_up - sum_up) / root
    ds_down = (quant_down * inv_down - sum_down) / root
    sums = jnp.stack([is_mine * ds_up, is_mine * ds_down])
    distance = 1
    while distance < peers:
        sums = sums + swap(sums, distance)
        distance *= 2

    pre_a = rounded(part_sum(dot(rows_a, q_up)))
    hidden_a = (pre_a * jax.nn.sigmoid(pre_a)).astype(jnp.bfloat16)
    outputs = dot(hidden_a, q_down).astype(jnp.bfloat16)

    grad = dot(hot_b, back)
    x_wide = x_b.astype(jnp.float32)
    inner = token_sum(jnp.sum(x_wide * grad, axis=1, keepdims=True))
    pull = rms_b * rms_b * rms_b * inner / width
    grad_in = c_b.astype(jnp.float32) + (rms_b * grad - x_wide * pull)
    next_cot = pass_on(grad_in.astype(jnp.bfloat16), -1)

    done_a = jnp.concatenate(exchange(split(outputs)), axis=0)
    mixed = x_a.astype(jnp.float32)
    for j, h in enumerate(hots_a):
        mixed = mixed + gates_ga[:, j : j + 1] * dot(h, done_a)
    next_a = pass_on(mixed.astype(jnp.bfloat16), 1)
    return (
        next_a[None],
        next_cot[None],
        dw_up[None],
        dw_down[None],
        sums[0][None],
        sums[1][None],
    )


def solution(mesh):
    tokens = P("pipe", "expert", None)
    columns = P("pipe", None, "expert")
    steps = P("pipe", None)
    return jax.shard_map(
        shards,
        mesh=mesh,
        in_specs=(tokens,) * 8 + (columns, steps, steps),
        out_specs=(tokens, tokens, tokens, columns, steps, steps),
        check_vma=False,
    )
```

```python
import math

import jax
import jax.numpy as jnp
from jax import lax
from jax.sharding import PartitionSpec as P

EXPERTS = 4
CAP = 34
CHUNKS = 4


qlimit = 7.0
epsilon = 1e-06

F_POLY = (3.99999827, -10.31875998, 10.67036777, -6.06749521, 1.94699036)
W_POLY = (19.73920584, -64.93916223, 85.45076959, -60.17190643, 25.98146098, -6.54589238)


def horner(coefs, z):
    acc = jnp.full_like(z, coefs[-1])
    for c in coefs[-2::-1]:
        acc = acc * z + c
    return acc


def reduced(weights, inv_scale):
    u = jnp.clip(weights.astype(jnp.float32) * inv_scale, -qlimit, qlimit)
    return u, u - jnp.round(u)


def fake_quant(weights, scale, inv_scale):
    u, r = reduced(weights, inv_scale)
    z = r * r
    return (scale * (u - r * ((0.25 - z) * horner(F_POLY, z)))).astype(jnp.bfloat16)


def quant_grads(weights, inv_scale, grads):
    u, r = reduced(weights, inv_scale)
    z = r * r
    weight_grad = grads * (z * horner(W_POLY, z))
    return weight_grad.astype(jnp.bfloat16), jnp.sum(weight_grad * u)


def dot(a, b, dims=(((1,), (0,)), ((), ()))):
    return lax.dot_general(a, b, dims, preferred_element_type=jnp.float32)


def rounded(value):
    return lax.reduce_precision(value, exponent_bits=8, mantissa_bits=7)


def after(value, *others):
    return lax.optimization_barrier((value, others))[0]


LAST = (((1,), (1,)), ((), ()))
FIRST = (((0,), (0,)), ((), ()))


def section(
    acts_a,
    acts_b,
    cot_b,
    routes_a,
    gates_a,
    routes_b,
    gates_b,
    up_weight,
    down_weight,
    up_scale,
    down_scale,
):
    peers = lax.axis_size("expert")
    stages = lax.axis_size("pipe")
    parts = peers // EXPERTS
    device_id = lax.axis_index("expert")
    expert_id = device_id // parts
    part_id = device_id % parts
    tokens, width = acts_a.shape[1], acts_a.shape[2]
    part_width = width // parts

    def swap(value, distance):
        return lax.ppermute(value, "expert", [(i, i ^ distance) for i in range(peers)])

    def part_sum(value):
        distance = 1
        while distance < parts:
            value = value + swap(value, distance)
            distance *= 2
        return value

    def token_sum(value):
        distance = 1
        while distance < parts:
            other = jnp.split(swap(value, distance), parts, axis=0)
            value = value + jnp.concatenate([other[k ^ distance] for k in range(parts)], axis=0)
            distance *= 2
        return value

    def spread(value):
        pieces = []
        for k in range(parts):
            start = (part_id ^ k) * part_width
            piece = lax.dynamic_slice_in_dim(value, start, part_width, axis=1)
            pieces.append(swap(piece, k) if k else piece)
        return jnp.concatenate(pieces, axis=0)

    def share(value):
        pieces = [swap(value, k) if k else value for k in range(parts)]
        return jnp.concatenate(pieces, axis=0)

    def exchange(blocks):
        return [swap(b, k * parts) if k else b for k, b in enumerate(blocks)]

    def pass_on(value, by):
        pieces = []
        for k in range(parts):
            block = value[k * tokens : (k + 1) * tokens]
            pairs = [
                (s * peers + i, (s + by) * peers + (i ^ k))
                for s in range(stages)
                if 0 <= s + by < stages
                for i in range(peers)
            ]
            pieces.append(lax.ppermute(block, ("pipe", "expert"), pairs))
        return pieces

    def in_columns(chunks):
        columns = []
        for q in range(parts):
            for pieces in chunks:
                column = pieces[0]
                for k in range(1, parts):
                    column = jnp.where((part_id ^ k) == q, pieces[k], column)
                columns.append(column)
        return jnp.concatenate(columns, axis=1)

    def one_hots(routes):
        near = jnp.bitwise_xor(routes, expert_id)
        matches = (near[:, :, None] == jnp.arange(EXPERTS)).astype(jnp.float32)
        both = matches.sum(1)
        lower = (jnp.arange(tokens)[:, None] > jnp.arange(tokens)[None, :]).astype(jnp.float32)
        earlier = dot(lower, both)
        chosen, seen = [], earlier
        for j in range(routes.shape[1]):
            m = matches[:, j]
            slot = jnp.sum(m * seen, axis=1)
            at_slot = (slot[:, None] == jnp.arange(CAP, dtype=jnp.float32)).astype(jnp.float32)
            chosen.append(m[:, :, None] * at_slot[:, None, :])
            seen = seen + m
        return chosen

    def group_hots(routes):
        hots = []
        for block in range(parts):
            hots.append(one_hots(routes[block * tokens : (block + 1) * tokens]))
        out = []
        for j in range(routes.shape[1]):
            rows = []
            for block in range(parts):
                here = (jnp.arange(parts) == (part_id ^ block)).astype(jnp.float32)
                rows.append(hots[block][j][:, :, None, :] * here[None, None, :, None])
            out.append(jnp.concatenate(rows, axis=0).reshape(parts * tokens, -1))
        return out

    def pack(hot, values):
        return dot(hot, values, FIRST)

    def split(rows):
        return jnp.split(rows, EXPERTS, axis=0)

    is_mine = (jnp.arange(EXPERTS, dtype=jnp.int32) == expert_id).astype(jnp.float32)
    s_up = jnp.sum(is_mine * up_scale[0])
    s_down = jnp.sum(is_mine * down_scale[0])
    inv_up, inv_down = 1.0 / s_up, 1.0 / s_down
    w_up, w_down = up_weight[0], down_weight[0]

    def inv_rms(x):
        wide = x.astype(jnp.float32)
        return lax.rsqrt(jnp.mean(wide * wide, axis=-1, keepdims=True) + epsilon)

    small = jnp.concatenate(
        [
            routes_b[0].astype(jnp.float32),
            gates_b[0],
            inv_rms(acts_b[0]),
            routes_a[0].astype(jnp.float32),
            gates_a[0],
            inv_rms(acts_a[0]),
        ],
        axis=1,
    )
    small = share(small)
    top = routes_a.shape[2]
    routes_gb, gates_gb, rms_b, routes_ga, gates_ga, rms_a = jnp.split(
        small, [top, 2 * top, 2 * top + 1, 3 * top + 1, 4 * top + 1], axis=1
    )
    x_b, c_b, x_a = spread(acts_b[0]), spread(cot_b[0]), spread(acts_a[0])

    hots_b = group_hots(routes_gb.astype(jnp.int32))
    hot_b = sum(hots_b).astype(jnp.bfloat16)
    gate_b = sum(jnp.sum(h * gates_gb[:, j : j + 1], axis=0) for j, h in enumerate(hots_b))
    norm_b = (x_b.astype(jnp.float32) * rms_b).astype(jnp.bfloat16)
    send_u = pack(hot_b, norm_b).astype(jnp.bfloat16)
    rows_u = jnp.concatenate(exchange(split(send_u)), axis=0)
    send_c = (pack(hot_b, after(c_b, send_u)) * gate_b[:, None]).astype(jnp.bfloat16)
    rows_c = jnp.concatenate(exchange(split(send_c)), axis=0)

    q_up = fake_quant(after(w_up, send_c), s_up, inv_up)
    q_down = fake_quant(after(w_down, q_up), s_down, inv_down)
    x_a = after(x_a, q_down)
    hots_a = [h.astype(jnp.bfloat16) for h in group_hots(routes_ga.astype(jnp.int32))]
    norm_a = (x_a.astype(jnp.float32) * rms_a).astype(jnp.bfloat16)
    send_a = pack(sum(hots_a), norm_a).astype(jnp.bfloat16)
    blocks_a = exchange(split(send_a))

    q_up, q_down = lax.optimization_barrier((q_up, q_down, send_a))[:2]

    own_pre_b = dot(rows_u, q_up)
    pre_b = rounded(part_sum(own_pre_b))
    own_grad = dot(rows_c, q_down, LAST)
    hidden_grad = rounded(part_sum(own_grad))
    sigma = jax.nn.sigmoid(pre_b)
    hidden_b = (pre_b * sigma).astype(jnp.bfloat16)
    pre_grad = (hidden_grad * sigma * (1.0 + pre_b * (1.0 - sigma))).astype(jnp.bfloat16)
    input_rows = dot(pre_grad, q_up, LAST).astype(jnp.bfloat16)
    back = jnp.concatenate(exchange(split(input_rows)), axis=0)

    rows_u, rows_c, own_pre_b, own_grad = lax.optimization_barrier(
        (rows_u, rows_c, own_pre_b, own_grad, input_rows)
    )[:4]
    dw_up, sum_up = quant_grads(w_up, inv_up, dot(rows_u, pre_grad, FIRST))
    dw_down, sum_down = quant_grads(w_down, inv_down, dot(hidden_b, rows_c, FIRST))
    quant_up = jnp.sum(pre_grad.astype(jnp.float32) * own_pre_b)
    quant_down = jnp.sum(hidden_b.astype(jnp.float32) * own_grad)
    root = math.sqrt(w_up.size * parts * qlimit)
    ds_up = (quant_up * inv_up - sum_up) / root
    ds_down = (quant_down * inv_down - sum_down) / root
    sums = jnp.stack([is_mine * ds_up, is_mine * ds_down])
    for c in range(peers.bit_length() - 1):
        sums = sums + swap(sums, 1 << c)

    rows_a = jnp.concatenate(after(blocks_a, dw_up, dw_down), axis=0)
    own_pre_a = dot(rows_a, q_up)
    pre_a = rounded(part_sum(own_pre_a))
    hidden_a = (pre_a * jax.nn.sigmoid(pre_a)).astype(jnp.bfloat16)
    pieces = CHUNKS
    step = part_width // pieces
    chunks = []
    for c in range(pieces):
        outputs = dot(hidden_a, q_down[:, c * step : (c + 1) * step]).astype(jnp.bfloat16)
        chunks.append(exchange(split(outputs)))

    grad = dot(hot_b, back)
    x_wide = x_b.astype(jnp.float32)
    own_inner = jnp.sum(x_wide * grad, axis=1, keepdims=True)
    inner = token_sum(own_inner)
    pull = rms_b * rms_b * rms_b * inner / width
    grad_in = c_b.astype(jnp.float32) + (rms_b * grad - x_wide * pull)
    next_cot = in_columns([pass_on(grad_in.astype(jnp.bfloat16), -1)])

    passed = []
    for c in range(pieces):
        done_a = jnp.concatenate(chunks[c], axis=0)
        mixed = x_a[:, c * step : (c + 1) * step].astype(jnp.float32)
        for j, h in enumerate(hots_a):
            mixed = mixed + gates_ga[:, j : j + 1] * dot(h, done_a)
        passed.append(pass_on(mixed.astype(jnp.bfloat16), 1))
    next_a = in_columns(passed)
    return (
        next_a[None],
        next_cot[None],
        dw_up[None],
        dw_down[None],
        sums[0][None],
        sums[1][None],
    )


def solution(mesh):
    tokens = P("pipe", "expert", None)
    columns = P("pipe", None, "expert")
    steps = P("pipe", None)
    return jax.shard_map(
        section,
        mesh=mesh,
        in_specs=(tokens,) * 8 + (columns, steps, steps),
        out_specs=(tokens, tokens, tokens, columns, steps, steps),
        check_vma=False,
    )
```

```python
import math

import jax
import jax.numpy as jnp
from jax import lax
from jax.sharding import PartitionSpec as P

EXPERTS = 4
CAP = 34
CHUNKS = 3


qlimit = 7.0
epsilon = 1e-06

F_POLY = (3.99999827, -10.31875998, 10.67036777, -6.06749521, 1.94699036)
W_POLY = (19.73920584, -64.93916223, 85.45076959, -60.17190643, 25.98146098, -6.54589238)


def horner(coefs, z):
    acc = jnp.full_like(z, coefs[-1])
    for c in coefs[-2::-1]:
        acc = acc * z + c
    return acc


def reduced(weights, inv_scale):
    u = jnp.clip(weights.astype(jnp.float32) * inv_scale, -qlimit, qlimit)
    return u, u - jnp.round(u)


def fake_quant(weights, scale, inv_scale):
    u, r = reduced(weights, inv_scale)
    z = r * r
    soft = u - r * ((0.25 - z) * horner(F_POLY, z))
    wave = z * horner(W_POLY, z)
    return tuple(t.astype(jnp.bfloat16) for t in (scale * soft, wave, soft - u * wave))


def quant_grads(wave, slope, grads):
    weight_grad = grads * wave.astype(jnp.float32)
    return weight_grad.astype(jnp.bfloat16), jnp.sum(grads * slope.astype(jnp.float32))


def dot(a, b, dims=(((1,), (0,)), ((), ()))):
    return lax.dot_general(a, b, dims, preferred_element_type=jnp.float32)


def rounded(value):
    return lax.reduce_precision(value, exponent_bits=8, mantissa_bits=7)


def after(value, *others):
    return lax.optimization_barrier((value, others))[0]


LAST = (((1,), (1,)), ((), ()))
FIRST = (((0,), (0,)), ((), ()))


def section(
    acts_a,
    acts_b,
    cot_b,
    routes_a,
    gates_a,
    routes_b,
    gates_b,
    up_weight,
    down_weight,
    up_scale,
    down_scale,
):
    peers = lax.axis_size("expert")
    stages = lax.axis_size("pipe")
    parts = peers // EXPERTS
    device_id = lax.axis_index("expert")
    expert_id = device_id // parts
    part_id = device_id % parts
    tokens, width = acts_a.shape[1], acts_a.shape[2]
    part_width = width // parts

    def swap(value, distance):
        return lax.ppermute(value, "expert", [(i, i ^ distance) for i in range(peers)])

    def part_sum(value):
        distance = 1
        while distance < parts:
            value = value + swap(value, distance)
            distance *= 2
        return value

    def token_sum(value):
        distance = 1
        while distance < parts:
            other = jnp.split(swap(value, distance), parts, axis=0)
            value = value + jnp.concatenate([other[k ^ distance] for k in range(parts)], axis=0)
            distance *= 2
        return value

    def columns_of(value, part):
        if parts == 2:
            return jnp.where(part == 0, value[:, :part_width], value[:, part_width:])
        return lax.dynamic_slice_in_dim(value, part * part_width, part_width, axis=1)

    def spread(value):
        pieces = [columns_of(value, part_id ^ k) for k in range(parts)]
        pieces = [swap(piece, k) if k else piece for k, piece in enumerate(pieces)]
        return jnp.concatenate(pieces, axis=0)

    def share(value):
        pieces = [swap(value, k) if k else value for k in range(parts)]
        return jnp.concatenate(pieces, axis=0)

    def exchange(blocks):
        return [swap(b, k * parts) if k else b for k, b in enumerate(blocks)]

    def pass_on(value, by):
        pieces = []
        for k in range(parts):
            block = value[k * tokens : (k + 1) * tokens]
            pairs = [
                (s * peers + i, (s + by) * peers + (i ^ k))
                for s in range(stages)
                if 0 <= s + by < stages
                for i in range(peers)
            ]
            pieces.append(lax.ppermute(block, ("pipe", "expert"), pairs))
        return pieces

    def in_columns(chunks):
        columns = []
        for q in range(parts):
            for pieces in chunks:
                column = pieces[0]
                for k in range(1, parts):
                    column = jnp.where((part_id ^ k) == q, pieces[k], column)
                columns.append(column)
        return jnp.concatenate(columns, axis=1)

    def slot_hots(routes):
        near = jnp.bitwise_xor(routes, expert_id)
        matches = (near[:, :, None] == jnp.arange(EXPERTS)).astype(jnp.bfloat16)
        place = jnp.arange(parts * tokens)
        block = place // tokens
        ahead = (place[:, None] > place[None, :]) & (block[:, None] == block[None, :])
        earlier = dot(ahead.astype(jnp.bfloat16), matches.sum(1).astype(jnp.bfloat16))
        first = jnp.bitwise_xor(block, part_id) * CAP
        hots = []
        for j in range(routes.shape[1]):
            slot = jnp.sum(matches[:, j].astype(jnp.float32) * earlier, axis=1).astype(jnp.int32)
            row = near[:, j] * (parts * CAP) + first + slot
            hots.append(row[:, None] == jnp.arange(EXPERTS * parts * CAP))
        return hots

    def pack(hot, values):
        return dot(hot, values, FIRST)

    def split(rows):
        return jnp.split(rows, EXPERTS, axis=0)

    is_mine = (jnp.arange(EXPERTS, dtype=jnp.int32) == expert_id).astype(jnp.float32)
    s_up = jnp.sum(is_mine * up_scale[0])
    s_down = jnp.sum(is_mine * down_scale[0])
    inv_up, inv_down = 1.0 / s_up, 1.0 / s_down
    w_up, w_down = up_weight[0], down_weight[0]

    def inv_rms(x):
        wide = x.astype(jnp.float32)
        return lax.rsqrt(jnp.mean(wide * wide, axis=-1, keepdims=True) + epsilon)

    top = routes_a.shape[2]
    small = share(jnp.concatenate([routes_b[0].astype(jnp.float32), gates_b[0]], axis=1))
    routes_gb, gates_gb = small[:, :top], small[:, top:]
    own_rms_b = inv_rms(acts_b[0])
    norm_b = spread((acts_b[0].astype(jnp.float32) * own_rms_b).astype(jnp.bfloat16))
    c_b = spread(cot_b[0])

    hots_b = slot_hots(routes_gb.astype(jnp.int32))
    hot_b = sum(h.astype(jnp.bfloat16) for h in hots_b)
    send_u = pack(hot_b, norm_b).astype(jnp.bfloat16)
    rows_u = jnp.concatenate(exchange(split(send_u)), axis=0)
    gate_b = sum(
        jnp.sum(jnp.where(h, gates_gb[:, j : j + 1], 0.0), axis=0) for j, h in enumerate(hots_b)
    )
    send_c = (pack(hot_b, after(c_b, send_u)) * gate_b[:, None]).astype(jnp.bfloat16)
    blocks_c = exchange(split(send_c))

    later_b, later_a, routes_a, gates_a, own_rms_b = after(
        (acts_b[0], acts_a[0], routes_a[0], gates_a[0], own_rms_b), send_c
    )
    small = jnp.concatenate(
        [routes_a.astype(jnp.float32), gates_a, inv_rms(later_a), own_rms_b], axis=1
    )
    small = share(small)
    x_a, x_b = spread(later_a), spread(later_b)
    routes_ga, gates_ga, rms_a, rms_b = jnp.split(small, [top, 2 * top, 2 * top + 1], axis=1)

    q_up, *slopes_up = fake_quant(after(w_up, send_c), s_up, inv_up)
    q_down, *slopes_down = fake_quant(after(w_down, q_up), s_down, inv_down)
    x_a = after(x_a, q_up)
    hots_a = [h.astype(jnp.bfloat16) for h in slot_hots(routes_ga.astype(jnp.int32))]
    norm_a = (x_a.astype(jnp.float32) * rms_a).astype(jnp.bfloat16)
    send_a = pack(sum(hots_a), norm_a).astype(jnp.bfloat16)
    blocks_a = exchange(split(send_a))

    q_up, q_down, slopes_up, slopes_down = lax.optimization_barrier(
        (q_up, q_down, slopes_up, slopes_down, send_a)
    )[:4]

    own_pre_b = dot(rows_u, q_up)
    pre_b = rounded(part_sum(own_pre_b))
    rows_c = jnp.concatenate(after(blocks_c, pre_b), axis=0)
    own_grad = dot(rows_c, q_down, LAST)
    hidden_grad = rounded(part_sum(own_grad))
    sigma = jax.nn.sigmoid(pre_b)
    hidden_b = (pre_b * sigma).astype(jnp.bfloat16)
    pre_grad = (hidden_grad * sigma * (1.0 + pre_b * (1.0 - sigma))).astype(jnp.bfloat16)
    input_rows = dot(pre_grad, q_up, LAST).astype(jnp.bfloat16)
    back = jnp.concatenate(exchange(split(input_rows)), axis=0)

    rows_u, rows_c = lax.optimization_barrier((rows_u, rows_c, input_rows))[:2]
    dw_up, sum_up = quant_grads(*slopes_up, dot(rows_u, pre_grad, FIRST))
    dw_down, sum_down = quant_grads(*slopes_down, dot(hidden_b, rows_c, FIRST))
    root = math.sqrt(w_up.size * parts * qlimit)
    ds_up, ds_down = sum_up / root, sum_down / root
    sums = jnp.stack([is_mine * ds_up, is_mine * ds_down])
    for c in range(peers.bit_length() - 1):
        sums = sums + swap(sums, 1 << c)

    rows_a = jnp.concatenate(after(blocks_a, dw_up, dw_down), axis=0)
    own_pre_a = dot(rows_a, q_up)
    pre_a = rounded(part_sum(own_pre_a))
    hidden_a = (pre_a * jax.nn.sigmoid(pre_a)).astype(jnp.bfloat16)
    lanes = 128 if part_width % 128 == 0 and part_width >= 128 * CHUNKS else 1
    units = part_width // lanes
    edges = [lanes * (-(-units * c // CHUNKS)) for c in range(CHUNKS + 1)]
    spans = list(zip(edges[:-1], edges[1:]))
    chunks = []
    for low, high in spans:
        outputs = dot(hidden_a, q_down[:, low:high]).astype(jnp.bfloat16)
        chunks.append(exchange(split(outputs)))

    grad = dot(hot_b, back)
    x_wide = x_b.astype(jnp.float32)
    own_inner = jnp.sum(x_wide * grad, axis=1, keepdims=True)
    inner = token_sum(own_inner)
    pull = rms_b * rms_b * rms_b * inner / width
    grad_in = c_b.astype(jnp.float32) + (rms_b * grad - x_wide * pull)
    next_cot = in_columns([pass_on(grad_in.astype(jnp.bfloat16), -1)])

    passed = []
    for c, (low, high) in enumerate(spans):
        done_a = jnp.concatenate(chunks[c], axis=0)
        mixed = x_a[:, low:high].astype(jnp.float32)
        for j, h in enumerate(hots_a):
            mixed = mixed + gates_ga[:, j : j + 1] * dot(h, done_a)
        passed.append(pass_on(mixed.astype(jnp.bfloat16), 1))
    next_a = in_columns(passed)
    return (
        next_a[None],
        next_cot[None],
        dw_up[None],
        dw_down[None],
        sums[0][None],
        sums[1][None],
    )


def solution(mesh):
    tokens = P("pipe", "expert", None)
    columns = P("pipe", None, "expert")
    steps = P("pipe", None)
    return jax.shard_map(
        section,
        mesh=mesh,
        in_specs=(tokens,) * 8 + (columns, steps, steps),
        out_specs=(tokens, tokens, tokens, columns, steps, steps),
        check_vma=False,
    )
```

```python
import math

import jax
import jax.numpy as jnp
from jax import lax
from jax.sharding import PartitionSpec as P

EXPERTS = 4
CAP = 34
CHUNKS = 3


qlimit = 7.0
epsilon = 1e-06

F_POLY = (3.99999827, -10.31875998, 10.67036777, -6.06749521, 1.94699036)
W_POLY = (19.73920584, -64.93916223, 85.45076959, -60.17190643, 25.98146098, -6.54589238)


def horner(coefs, z):
    acc = jnp.full_like(z, coefs[-1])
    for c in coefs[-2::-1]:
        acc = acc * z + c
    return acc


def reduced(weights, inv_scale):
    u = jnp.clip(weights.astype(jnp.float32) * inv_scale, -qlimit, qlimit)
    return u, u - jnp.round(u)


def fake_quant(weights, scale, inv_scale):
    u, r = reduced(weights, inv_scale)
    z = r * r
    soft = u - r * ((0.25 - z) * horner(F_POLY, z))
    wave = z * horner(W_POLY, z)
    return tuple(t.astype(jnp.bfloat16) for t in (scale * soft, wave, soft - u * wave))


def quant_grads(wave, slope, grads):
    weight_grad = grads * wave.astype(jnp.float32)
    return weight_grad.astype(jnp.bfloat16), jnp.sum(grads * slope.astype(jnp.float32))


def dot(a, b, dims=(((1,), (0,)), ((), ()))):
    return lax.dot_general(a, b, dims, preferred_element_type=jnp.float32)


def rounded(value):
    return lax.reduce_precision(value, exponent_bits=8, mantissa_bits=7)


def after(value, *others):
    return lax.optimization_barrier((value, others))[0]


LAST = (((1,), (1,)), ((), ()))
FIRST = (((0,), (0,)), ((), ()))


def section(
    acts_a,
    acts_b,
    cot_b,
    routes_a,
    gates_a,
    routes_b,
    gates_b,
    up_weight,
    down_weight,
    up_scale,
    down_scale,
):
    peers = lax.axis_size("expert")
    stages = lax.axis_size("pipe")
    parts = peers // EXPERTS
    device_id = lax.axis_index("expert")
    expert_id = device_id // parts
    part_id = device_id % parts
    tokens, width = acts_a.shape[1], acts_a.shape[2]
    part_width = width // parts

    def swap(value, distance):
        return lax.ppermute(value, "expert", [(i, i ^ distance) for i in range(peers)])

    def part_sum(value):
        distance = 1
        while distance < parts:
            value = value + swap(value, distance)
            distance *= 2
        return value

    def token_sum(value):
        distance = 1
        while distance < parts:
            other = jnp.split(swap(value, distance), parts, axis=0)
            value = value + jnp.concatenate([other[k ^ distance] for k in range(parts)], axis=0)
            distance *= 2
        return value

    def columns_of(value, part):
        if parts == 2:
            return jnp.where(part == 0, value[:, :part_width], value[:, part_width:])
        return lax.dynamic_slice_in_dim(value, part * part_width, part_width, axis=1)

    def spread(value):
        pieces = [columns_of(value, part_id ^ k) for k in range(parts)]
        pieces = [swap(piece, k) if k else piece for k, piece in enumerate(pieces)]
        return jnp.concatenate(pieces, axis=0)

    def share(value):
        pieces = [swap(value, k) if k else value for k in range(parts)]
        return jnp.concatenate(pieces, axis=0)

    def exchange(blocks):
        return [swap(b, k * parts) if k else b for k, b in enumerate(blocks)]

    def pass_on(value, by):
        pieces = []
        for k in range(parts):
            block = value[k * tokens : (k + 1) * tokens]
            pairs = [
                (s * peers + i, (s + by) * peers + (i ^ k))
                for s in range(stages)
                if 0 <= s + by < stages
                for i in range(peers)
            ]
            pieces.append(lax.ppermute(block, ("pipe", "expert"), pairs))
        return pieces

    def in_columns(chunks):
        columns = []
        for q in range(parts):
            for pieces in chunks:
                column = pieces[0]
                for k in range(1, parts):
                    column = jnp.where((part_id ^ k) == q, pieces[k], column)
                columns.append(column)
        return jnp.concatenate(columns, axis=1)

    def slot_hots(routes):
        near = jnp.bitwise_xor(routes, expert_id)
        matches = (near[:, :, None] == jnp.arange(EXPERTS)).astype(jnp.bfloat16)
        place = jnp.arange(parts * tokens)
        block = place // tokens
        ahead = (place[:, None] > place[None, :]) & (block[:, None] == block[None, :])
        earlier = dot(ahead.astype(jnp.bfloat16), matches.sum(1).astype(jnp.bfloat16))
        first = jnp.bitwise_xor(block, part_id) * CAP
        hots = []
        for j in range(routes.shape[1]):
            slot = jnp.sum(matches[:, j].astype(jnp.float32) * earlier, axis=1).astype(jnp.int32)
            row = near[:, j] * (parts * CAP) + first + slot
            hots.append(row[:, None] == jnp.arange(EXPERTS * parts * CAP))
        return hots

    def pack(hot, values):
        return dot(hot, values, FIRST)

    def split(rows):
        return jnp.split(rows, EXPERTS, axis=0)

    is_mine = (jnp.arange(EXPERTS, dtype=jnp.int32) == expert_id).astype(jnp.float32)
    s_up = jnp.sum(is_mine * up_scale[0])
    s_down = jnp.sum(is_mine * down_scale[0])
    inv_up, inv_down = 1.0 / s_up, 1.0 / s_down
    w_up, w_down = up_weight[0], down_weight[0]

    def inv_rms(x):
        wide = x.astype(jnp.float32)
        return lax.rsqrt(jnp.mean(wide * wide, axis=-1, keepdims=True) + epsilon)

    top = routes_a.shape[2]
    small = share(jnp.concatenate([routes_b[0].astype(jnp.float32), gates_b[0]], axis=1))
    routes_gb, gates_gb = small[:, :top], small[:, top:]
    own_rms_b = inv_rms(acts_b[0])
    norm_b = spread((acts_b[0].astype(jnp.float32) * own_rms_b).astype(jnp.bfloat16))
    c_b = spread(cot_b[0])

    hots_b = slot_hots(routes_gb.astype(jnp.int32))
    hot_b = sum(h.astype(jnp.bfloat16) for h in hots_b)
    send_u = pack(hot_b, norm_b).astype(jnp.bfloat16)
    rows_u = jnp.concatenate(exchange(split(send_u)), axis=0)
    gate_b = sum(
        jnp.sum(jnp.where(h, gates_gb[:, j : j + 1], 0.0), axis=0) for j, h in enumerate(hots_b)
    )
    send_c = (pack(hot_b, after(c_b, send_u)) * gate_b[:, None]).astype(jnp.bfloat16)
    blocks_c = exchange(split(send_c))

    later_b, later_a, routes_a, gates_a, own_rms_b = after(
        (acts_b[0], acts_a[0], routes_a[0], gates_a[0], own_rms_b), send_c
    )
    small = jnp.concatenate(
        [routes_a.astype(jnp.float32), gates_a, inv_rms(later_a), own_rms_b], axis=1
    )
    small = share(small)
    x_a, x_b = spread(later_a), spread(later_b)
    routes_ga, gates_ga, rms_a, rms_b = jnp.split(small, [top, 2 * top, 2 * top + 1], axis=1)

    q_up, *slopes_up = fake_quant(after(w_up, send_c), s_up, inv_up)
    q_down, *slopes_down = fake_quant(after(w_down, q_up), s_down, inv_down)
    x_a = after(x_a, q_up)
    hots_a = [h.astype(jnp.bfloat16) for h in slot_hots(routes_ga.astype(jnp.int32))]
    norm_a = (x_a.astype(jnp.float32) * rms_a).astype(jnp.bfloat16)
    send_a = pack(sum(hots_a), norm_a).astype(jnp.bfloat16)
    blocks_a = exchange(split(send_a))

    q_up, q_down, slopes_up, slopes_down = lax.optimization_barrier(
        (q_up, q_down, slopes_up, slopes_down, send_a)
    )[:4]

    own_pre_b = dot(rows_u, q_up)
    pre_b = rounded(part_sum(own_pre_b))
    rows_c = jnp.concatenate(after(blocks_c, pre_b), axis=0)
    own_grad = dot(rows_c, q_down, LAST)
    hidden_grad = rounded(part_sum(own_grad))
    sigma = jax.nn.sigmoid(pre_b)
    hidden_b = (pre_b * sigma).astype(jnp.bfloat16)
    pre_grad = (hidden_grad * sigma * (1.0 + pre_b * (1.0 - sigma))).astype(jnp.bfloat16)
    input_rows = dot(pre_grad, q_up, LAST).astype(jnp.bfloat16)
    blocks_back = exchange(split(input_rows))
    back = jnp.concatenate(blocks_back, axis=0)

    rows_u, rows_c = lax.optimization_barrier((rows_u, rows_c, input_rows))[:2]
    dw_up, sum_up = quant_grads(*slopes_up, dot(rows_u, pre_grad, FIRST))
    dw_down, sum_down = quant_grads(*slopes_down, dot(hidden_b, rows_c, FIRST))
    root = math.sqrt(w_up.size * parts * qlimit)
    ds_up, ds_down = sum_up / root, sum_down / root
    sums = jnp.stack([is_mine * ds_up, is_mine * ds_down])
    for c in range(peers.bit_length() - 1):
        sums = sums + swap(sums, 1 << c)

    rows_a = jnp.concatenate(after(blocks_a, dw_up, dw_down), axis=0)
    own_pre_a = dot(rows_a, q_up)
    pre_a = rounded(part_sum(own_pre_a))
    hidden_a = (pre_a * jax.nn.sigmoid(pre_a)).astype(jnp.bfloat16)
    lanes = 128 if part_width % 128 == 0 and part_width >= 128 * CHUNKS else 1
    units = part_width // lanes
    edges = [lanes * (-(-units * c // CHUNKS)) for c in range(CHUNKS + 1)]
    spans = list(zip(edges[:-1], edges[1:]))
    chunks = []
    for c, (low, high) in enumerate(spans):
        outputs = dot(hidden_a, q_down[:, low:high]).astype(jnp.bfloat16)
        if c == 0:
            outputs = after(outputs, blocks_back[3])
        chunks.append(exchange(split(outputs)))

    grad = dot(hot_b, back)
    x_wide = x_b.astype(jnp.float32)
    own_inner = jnp.sum(x_wide * grad, axis=1, keepdims=True)
    inner = token_sum(own_inner)
    pull = rms_b * rms_b * rms_b * inner / width
    grad_in = c_b.astype(jnp.float32) + (rms_b * grad - x_wide * pull)
    next_cot = in_columns([pass_on(grad_in.astype(jnp.bfloat16), -1)])

    passed = []
    for c, (low, high) in enumerate(spans):
        done_a = jnp.concatenate(chunks[c], axis=0)
        mixed = x_a[:, low:high].astype(jnp.float32)
        for j, h in enumerate(hots_a):
            mixed = mixed + gates_ga[:, j : j + 1] * dot(h, done_a)
        passed.append(pass_on(mixed.astype(jnp.bfloat16), 1))
    next_a = in_columns(passed)
    return (
        next_a[None],
        next_cot[None],
        dw_up[None],
        dw_down[None],
        sums[0][None],
        sums[1][None],
    )


def solution(mesh):
    tokens = P("pipe", "expert", None)
    columns = P("pipe", None, "expert")
    steps = P("pipe", None)
    return jax.shard_map(
        section,
        mesh=mesh,
        in_specs=(tokens,) * 8 + (columns, steps, steps),
        out_specs=(tokens, tokens, tokens, columns, steps, steps),
        check_vma=False,
    )
```

```python
import math

import jax
import jax.numpy as jnp
from jax import lax
from jax.sharding import PartitionSpec as P

EXPERTS = 4
CAP = 34
CHUNKS = 3


qlimit = 7.0
epsilon = 1e-06

F_POLY = (3.99999827, -10.31875998, 10.67036777, -6.06749521, 1.94699036)
W_POLY = (19.73920584, -64.93916223, 85.45076959, -60.17190643, 25.98146098, -6.54589238)


def horner(coefs, z):
    acc = jnp.full_like(z, coefs[-1])
    for c in coefs[-2::-1]:
        acc = acc * z + c
    return acc


def reduced(weights, inv_scale):
    u = jnp.clip(weights.astype(jnp.float32) * inv_scale, -qlimit, qlimit)
    return u, u - jnp.round(u)


def fake_quant(weights, scale, inv_scale):
    u, r = reduced(weights, inv_scale)
    z = r * r
    soft = u - r * ((0.25 - z) * horner(F_POLY, z))
    wave = z * horner(W_POLY, z)
    return tuple(t.astype(jnp.bfloat16) for t in (scale * soft, wave, soft - u * wave))


def quant_grads(wave, slope, grads):
    weight_grad = grads * wave.astype(jnp.float32)
    return weight_grad.astype(jnp.bfloat16), jnp.sum(grads * slope.astype(jnp.float32))


def dot(a, b, dims=(((1,), (0,)), ((), ()))):
    return lax.dot_general(a, b, dims, preferred_element_type=jnp.float32)


def rounded(value):
    return lax.reduce_precision(value, exponent_bits=8, mantissa_bits=7)


def after(value, *others):
    return lax.optimization_barrier((value, others))[0]


LAST = (((1,), (1,)), ((), ()))
FIRST = (((0,), (0,)), ((), ()))


def section(
    acts_a,
    acts_b,
    cot_b,
    routes_a,
    gates_a,
    routes_b,
    gates_b,
    up_weight,
    down_weight,
    up_scale,
    down_scale,
):
    peers = lax.axis_size("expert")
    stages = lax.axis_size("pipe")
    parts = peers // EXPERTS
    device_id = lax.axis_index("expert")
    expert_id = device_id // parts
    part_id = device_id % parts
    tokens, width = acts_a.shape[1], acts_a.shape[2]
    part_width = width // parts

    def swap(value, distance):
        return lax.ppermute(value, "expert", [(i, i ^ distance) for i in range(peers)])

    def part_sum(value):
        distance = 1
        while distance < parts:
            value = value + swap(value, distance)
            distance *= 2
        return value

    def token_sum(value):
        distance = 1
        while distance < parts:
            other = jnp.split(swap(value, distance), parts, axis=0)
            value = value + jnp.concatenate([other[k ^ distance] for k in range(parts)], axis=0)
            distance *= 2
        return value

    def columns_of(value, part):
        if parts == 2:
            return jnp.where(part == 0, value[:, :part_width], value[:, part_width:])
        return lax.dynamic_slice_in_dim(value, part * part_width, part_width, axis=1)

    def spread(value):
        pieces = [columns_of(value, part_id ^ k) for k in range(parts)]
        pieces = [swap(piece, k) if k else piece for k, piece in enumerate(pieces)]
        return jnp.concatenate(pieces, axis=0)

    def share(value):
        pieces = [swap(value, k) if k else value for k in range(parts)]
        return jnp.concatenate(pieces, axis=0)

    def exchange(blocks):
        return [swap(b, k * parts) if k else b for k, b in enumerate(blocks)]

    def ahead(value):
        return lax.ppermute(value, "pipe", [(s, s + 1) for s in range(stages - 1)])

    def pass_on(value, by):
        pieces = []
        for k in range(parts):
            block = value[k * tokens : (k + 1) * tokens]
            pairs = [
                (s * peers + i, (s + by) * peers + (i ^ k))
                for s in range(stages)
                if 0 <= s + by < stages
                for i in range(peers)
            ]
            pieces.append(lax.ppermute(block, ("pipe", "expert"), pairs))
        return pieces

    def in_columns(chunks):
        columns = []
        for q in range(parts):
            for pieces in chunks:
                column = pieces[0]
                for k in range(1, parts):
                    column = jnp.where((part_id ^ k) == q, pieces[k], column)
                columns.append(column)
        return jnp.concatenate(columns, axis=1)

    def slot_hots(routes):
        near = jnp.bitwise_xor(routes, expert_id)
        matches = (near[:, :, None] == jnp.arange(EXPERTS)).astype(jnp.bfloat16)
        place = jnp.arange(parts * tokens)
        block = place // tokens
        ahead = (place[:, None] > place[None, :]) & (block[:, None] == block[None, :])
        earlier = dot(ahead.astype(jnp.bfloat16), matches.sum(1).astype(jnp.bfloat16))
        first = jnp.bitwise_xor(block, part_id) * CAP
        hots = []
        for j in range(routes.shape[1]):
            slot = jnp.sum(matches[:, j].astype(jnp.float32) * earlier, axis=1).astype(jnp.int32)
            row = near[:, j] * (parts * CAP) + first + slot
            hots.append(row[:, None] == jnp.arange(EXPERTS * parts * CAP))
        return hots

    def pack(hot, values):
        return dot(hot, values, FIRST)

    def split(rows):
        return jnp.split(rows, EXPERTS, axis=0)

    is_mine = (jnp.arange(EXPERTS, dtype=jnp.int32) == expert_id).astype(jnp.float32)
    s_up = jnp.sum(is_mine * up_scale[0])
    s_down = jnp.sum(is_mine * down_scale[0])
    inv_up, inv_down = 1.0 / s_up, 1.0 / s_down
    w_up, w_down = up_weight[0], down_weight[0]

    def inv_rms(x):
        wide = x.astype(jnp.float32)
        return lax.rsqrt(jnp.mean(wide * wide, axis=-1, keepdims=True) + epsilon)

    top = routes_a.shape[2]
    small = share(jnp.concatenate([routes_b[0].astype(jnp.float32), gates_b[0]], axis=1))
    routes_gb, gates_gb = small[:, :top], small[:, top:]
    own_rms_b = inv_rms(acts_b[0])
    norm_b = spread((acts_b[0].astype(jnp.float32) * own_rms_b).astype(jnp.bfloat16))
    c_b = spread(cot_b[0])

    hots_b = slot_hots(routes_gb.astype(jnp.int32))
    hot_b = sum(h.astype(jnp.bfloat16) for h in hots_b)
    send_u = pack(hot_b, norm_b).astype(jnp.bfloat16)
    rows_u = jnp.concatenate(exchange(split(send_u)), axis=0)
    gate_b = sum(
        jnp.sum(jnp.where(h, gates_gb[:, j : j + 1], 0.0), axis=0) for j, h in enumerate(hots_b)
    )
    send_c = (pack(hot_b, after(c_b, send_u)) * gate_b[:, None]).astype(jnp.bfloat16)
    blocks_c = exchange(split(send_c))

    later_b, later_a, routes_a, gates_a, own_rms_b = after(
        (acts_b[0], acts_a[0], routes_a[0], gates_a[0], own_rms_b), send_c
    )
    small = jnp.concatenate(
        [routes_a.astype(jnp.float32), gates_a, inv_rms(later_a), own_rms_b], axis=1
    )
    small = share(small)
    x_a, x_b = spread(later_a), spread(later_b)
    routes_ga, gates_ga, rms_a, rms_b = jnp.split(small, [top, 2 * top, 2 * top + 1], axis=1)

    q_up, *slopes_up = fake_quant(after(w_up, send_c), s_up, inv_up)
    q_down, *slopes_down = fake_quant(after(w_down, q_up), s_down, inv_down)
    lanes = 128 if part_width % 128 == 0 and part_width >= 128 * CHUNKS else 1
    units = part_width // lanes
    edges = [lanes * (-(-units * c // CHUNKS)) for c in range(CHUNKS + 1)]
    spans = list(zip(edges[:-1], edges[1:]))
    x_a = after(x_a, q_up)
    hots_a = [h.astype(jnp.bfloat16) for h in slot_hots(routes_ga.astype(jnp.int32))]
    low, high = spans[-1]
    next_x = ahead(x_a[:, low:high])
    routing = ahead(jnp.concatenate([routes_ga, gates_ga], axis=1))
    next_hots = slot_hots(routing[:, :top].astype(jnp.int32))
    sources = [(x_a[:, low:high], gates_ga, hots_a) for low, high in spans[:-1]]
    sources.append((next_x, routing[:, top:], [h.astype(jnp.bfloat16) for h in next_hots]))
    norm_a = (x_a.astype(jnp.float32) * rms_a).astype(jnp.bfloat16)
    send_a = pack(sum(hots_a), norm_a).astype(jnp.bfloat16)
    blocks_a = exchange(split(after(send_a, blocks_c[-1])))

    q_up, q_down, slopes_up, slopes_down = lax.optimization_barrier(
        (q_up, q_down, slopes_up, slopes_down, send_a)
    )[:4]

    own_pre_b = dot(rows_u, q_up)
    pre_b = rounded(part_sum(own_pre_b))
    rows_c = jnp.concatenate(after(blocks_c, pre_b), axis=0)
    own_grad = dot(rows_c, q_down, LAST)
    hidden_grad = rounded(part_sum(own_grad))
    sigma = jax.nn.sigmoid(pre_b)
    hidden_b = (pre_b * sigma).astype(jnp.bfloat16)
    pre_grad = (hidden_grad * sigma * (1.0 + pre_b * (1.0 - sigma))).astype(jnp.bfloat16)
    input_rows = dot(pre_grad, q_up, LAST).astype(jnp.bfloat16)
    blocks_back = exchange(split(input_rows))
    back = jnp.concatenate(blocks_back, axis=0)

    rows_u, rows_c = lax.optimization_barrier((rows_u, rows_c, input_rows))[:2]
    dw_up, sum_up = quant_grads(*slopes_up, dot(rows_u, pre_grad, FIRST))
    dw_down, sum_down = quant_grads(*slopes_down, dot(hidden_b, rows_c, FIRST))
    root = math.sqrt(w_up.size * parts * qlimit)
    ds_up, ds_down = sum_up / root, sum_down / root
    sums = jnp.stack([is_mine * ds_up, is_mine * ds_down])
    for c in range(peers.bit_length() - 1):
        sums = sums + swap(sums, 1 << c)

    rows_a = jnp.concatenate(after(blocks_a, dw_up, dw_down), axis=0)
    own_pre_a = dot(rows_a, q_up)
    pre_a = rounded(part_sum(own_pre_a))
    hidden_a = (pre_a * jax.nn.sigmoid(pre_a)).astype(jnp.bfloat16)
    ready = [None] * CHUNKS
    for c in (CHUNKS - 1, *range(CHUNKS - 1)):
        low, high = spans[c]
        ready[c] = dot(hidden_a, q_down[:, low:high]).astype(jnp.bfloat16)
    ready[-1] = ahead(ready[-1])
    ready[0] = after(ready[0], blocks_back[-1])
    chunks = [exchange(split(rows)) for rows in ready]

    grad = dot(hot_b, back)
    x_wide = x_b.astype(jnp.float32)
    own_inner = jnp.sum(x_wide * grad, axis=1, keepdims=True)
    inner = token_sum(own_inner)
    pull = rms_b * rms_b * rms_b * inner / width
    grad_in = c_b.astype(jnp.float32) + (rms_b * grad - x_wide * pull)
    next_cot = in_columns([pass_on(grad_in.astype(jnp.bfloat16), -1)])

    passed = []
    for c, (x_c, gates_c, hots_c) in enumerate(sources):
        done_a = jnp.concatenate(chunks[c], axis=0)
        mixed = x_c.astype(jnp.float32)
        for j, h in enumerate(hots_c):
            mixed = mixed + gates_c[:, j : j + 1] * dot(h, done_a)
        mixed = mixed.astype(jnp.bfloat16)
        if c < CHUNKS - 1:
            passed.append(pass_on(mixed, 1))
        else:
            pieces = jnp.split(mixed, parts, axis=0)
            passed.append([swap(piece, k) if k else piece for k, piece in enumerate(pieces)])
    next_a = in_columns(passed)
    return (
        next_a[None],
        next_cot[None],
        dw_up[None],
        dw_down[None],
        sums[0][None],
        sums[1][None],
    )


def solution(mesh):
    tokens = P("pipe", "expert", None)
    columns = P("pipe", None, "expert")
    steps = P("pipe", None)
    return jax.shard_map(
        section,
        mesh=mesh,
        in_specs=(tokens,) * 8 + (columns, steps, steps),
        out_specs=(tokens, tokens, tokens, columns, steps, steps),
        check_vma=False,
    )
```

```python
import math

import jax
import jax.numpy as jnp
from jax import lax
from jax.sharding import PartitionSpec as P

EXPERTS = 4
CAP = 34
CHUNKS = 3


qlimit = 7.0
epsilon = 1e-06

F_POLY = (3.99999827, -10.31875998, 10.67036777, -6.06749521, 1.94699036)
W_POLY = (19.73920584, -64.93916223, 85.45076959, -60.17190643, 25.98146098, -6.54589238)


def horner(coefs, z):
    acc = jnp.full_like(z, coefs[-1])
    for c in coefs[-2::-1]:
        acc = acc * z + c
    return acc


def reduced(weights, inv_scale):
    u = jnp.clip(weights.astype(jnp.float32) * inv_scale, -qlimit, qlimit)
    return u, u - jnp.round(u)


def fake_quant(weights, scale, inv_scale):
    u, r = reduced(weights, inv_scale)
    z = r * r
    soft = u - r * ((0.25 - z) * horner(F_POLY, z))
    wave = z * horner(W_POLY, z)
    return tuple(t.astype(jnp.bfloat16) for t in (scale * soft, wave, soft - u * wave))


def quant_grads(wave, slope, grads):
    weight_grad = grads * wave.astype(jnp.float32)
    return weight_grad.astype(jnp.bfloat16), jnp.sum(grads * slope.astype(jnp.float32))


def dot(a, b, dims=(((1,), (0,)), ((), ()))):
    return lax.dot_general(a, b, dims, preferred_element_type=jnp.float32)


def rounded(value):
    return lax.reduce_precision(value, exponent_bits=8, mantissa_bits=7)


def after(value, *others):
    return lax.optimization_barrier((value, others))[0]


LAST = (((1,), (1,)), ((), ()))
FIRST = (((0,), (0,)), ((), ()))


def section(
    acts_a,
    acts_b,
    cot_b,
    routes_a,
    gates_a,
    routes_b,
    gates_b,
    up_weight,
    down_weight,
    up_scale,
    down_scale,
):
    peers = lax.axis_size("expert")
    stages = lax.axis_size("pipe")
    parts = peers // EXPERTS
    device_id = lax.axis_index("expert")
    expert_id = device_id // parts
    part_id = device_id % parts
    tokens, width = acts_a.shape[1], acts_a.shape[2]
    part_width = width // parts

    def swap(value, distance):
        return lax.ppermute(value, "expert", [(i, i ^ distance) for i in range(peers)])

    def part_sum(value):
        distance = 1
        while distance < parts:
            value = value + swap(value, distance)
            distance *= 2
        return value

    def token_sum(value):
        distance = 1
        while distance < parts:
            other = jnp.split(swap(value, distance), parts, axis=0)
            value = value + jnp.concatenate([other[k ^ distance] for k in range(parts)], axis=0)
            distance *= 2
        return value

    def columns_of(value, part):
        if parts == 2:
            return jnp.where(part == 0, value[:, :part_width], value[:, part_width:])
        return lax.dynamic_slice_in_dim(value, part * part_width, part_width, axis=1)

    def spread(value):
        pieces = [columns_of(value, part_id ^ k) for k in range(parts)]
        pieces = [swap(piece, k) if k else piece for k, piece in enumerate(pieces)]
        return jnp.concatenate(pieces, axis=0)

    def share(value):
        pieces = [swap(value, k) if k else value for k in range(parts)]
        return jnp.concatenate(pieces, axis=0)

    def exchange(blocks):
        return [swap(b, k * parts) if k else b for k, b in enumerate(blocks)]

    def ahead(value):
        return lax.ppermute(value, "pipe", [(s, s + 1) for s in range(stages - 1)])

    def pass_on(value, by):
        pieces = []
        for k in range(parts):
            block = value[k * tokens : (k + 1) * tokens]
            pairs = [
                (s * peers + i, (s + by) * peers + (i ^ k))
                for s in range(stages)
                if 0 <= s + by < stages
                for i in range(peers)
            ]
            pieces.append(lax.ppermute(block, ("pipe", "expert"), pairs))
        return pieces

    def in_columns(chunks):
        columns = []
        for q in range(parts):
            for pieces in chunks:
                column = pieces[0]
                for k in range(1, parts):
                    column = jnp.where((part_id ^ k) == q, pieces[k], column)
                columns.append(column)
        return jnp.concatenate(columns, axis=1)

    def slot_hots(routes):
        near = jnp.bitwise_xor(routes, expert_id)
        matches = (near[:, :, None] == jnp.arange(EXPERTS)).astype(jnp.bfloat16)
        place = jnp.arange(parts * tokens)
        block = place // tokens
        ahead = (place[:, None] > place[None, :]) & (block[:, None] == block[None, :])
        earlier = dot(ahead.astype(jnp.bfloat16), matches.sum(1).astype(jnp.bfloat16))
        first = jnp.bitwise_xor(block, part_id) * CAP
        hots = []
        for j in range(routes.shape[1]):
            slot = jnp.sum(matches[:, j].astype(jnp.float32) * earlier, axis=1).astype(jnp.int32)
            row = near[:, j] * (parts * CAP) + first + slot
            hots.append(row[:, None] == jnp.arange(EXPERTS * parts * CAP))
        return hots

    def pack(hot, values):
        return dot(hot, values, FIRST)

    def split(rows):
        return jnp.split(rows, EXPERTS, axis=0)

    is_mine = (jnp.arange(EXPERTS, dtype=jnp.int32) == expert_id).astype(jnp.float32)
    s_up = jnp.sum(is_mine * up_scale[0])
    s_down = jnp.sum(is_mine * down_scale[0])
    inv_up, inv_down = 1.0 / s_up, 1.0 / s_down
    w_up, w_down = up_weight[0], down_weight[0]

    def inv_rms(x):
        wide = x.astype(jnp.float32)
        return lax.rsqrt(jnp.mean(wide * wide, axis=-1, keepdims=True) + epsilon)

    top = routes_a.shape[2]
    small = share(jnp.concatenate([routes_b[0].astype(jnp.float32), gates_b[0]], axis=1))
    routes_gb, gates_gb = small[:, :top], small[:, top:]
    own_rms_b = inv_rms(acts_b[0])
    norm_b = spread((acts_b[0].astype(jnp.float32) * own_rms_b).astype(jnp.bfloat16))
    c_b = spread(cot_b[0])

    hots_b = slot_hots(routes_gb.astype(jnp.int32))
    hot_b = sum(h.astype(jnp.bfloat16) for h in hots_b)
    send_u = pack(hot_b, norm_b).astype(jnp.bfloat16)
    rows_u = jnp.concatenate(exchange(split(send_u)), axis=0)
    gate_b = sum(
        jnp.sum(jnp.where(h, gates_gb[:, j : j + 1], 0.0), axis=0) for j, h in enumerate(hots_b)
    )
    send_c = (pack(hot_b, after(c_b, send_u)) * gate_b[:, None]).astype(jnp.bfloat16)
    blocks_c = exchange(split(send_c))

    later_b, later_a, routes_a, gates_a, own_rms_b = after(
        (acts_b[0], acts_a[0], routes_a[0], gates_a[0], own_rms_b), send_c
    )
    small = jnp.concatenate(
        [routes_a.astype(jnp.float32), gates_a, inv_rms(later_a), own_rms_b], axis=1
    )
    small = share(small)
    x_a, x_b = spread(later_a), spread(later_b)
    routes_ga, gates_ga, rms_a, rms_b = jnp.split(small, [top, 2 * top, 2 * top + 1], axis=1)

    q_up, *slopes_up = fake_quant(after(w_up, send_c), s_up, inv_up)
    q_down, *slopes_down = fake_quant(after(w_down, q_up), s_down, inv_down)
    lanes = 128 if part_width % 128 == 0 and part_width >= 128 * CHUNKS else 1
    units = part_width // lanes
    edges = [lanes * (-(-units * c // CHUNKS)) for c in range(CHUNKS + 1)]
    spans = list(zip(edges[:-1], edges[1:]))
    x_a = after(x_a, q_up)
    hots_a = [h.astype(jnp.bfloat16) for h in slot_hots(routes_ga.astype(jnp.int32))]
    low, high = spans[-1]
    next_x = ahead(x_a[:, low:high])
    routing = ahead(jnp.concatenate([routes_ga, gates_ga], axis=1))
    next_hots = slot_hots(routing[:, :top].astype(jnp.int32))
    sources = [(x_a[:, low:high], gates_ga, hots_a) for low, high in spans[:-1]]
    sources.append((next_x, routing[:, top:], [h.astype(jnp.bfloat16) for h in next_hots]))
    norm_a = (x_a.astype(jnp.float32) * rms_a).astype(jnp.bfloat16)
    send_a = pack(sum(hots_a), norm_a).astype(jnp.bfloat16)
    blocks_a = exchange(split(after(send_a, blocks_c[-1])))

    q_up, q_down, slopes_up, slopes_down = lax.optimization_barrier(
        (q_up, q_down, slopes_up, slopes_down, send_a)
    )[:4]

    own_pre_b = dot(rows_u, q_up)
    pre_b = rounded(part_sum(own_pre_b))
    rows_c = jnp.concatenate(after(blocks_c, pre_b), axis=0)
    own_grad = dot(rows_c, q_down, LAST)
    hidden_grad = rounded(part_sum(own_grad))
    sigma = jax.nn.sigmoid(pre_b)
    hidden_b = (pre_b * sigma).astype(jnp.bfloat16)
    pre_grad = (hidden_grad * sigma * (1.0 + pre_b * (1.0 - sigma))).astype(jnp.bfloat16)
    input_rows = dot(pre_grad, q_up, LAST).astype(jnp.bfloat16)
    blocks_back = exchange(split(input_rows))
    back = jnp.concatenate(blocks_back, axis=0)

    rows_u, rows_c = lax.optimization_barrier((rows_u, rows_c, input_rows))[:2]
    dw_up, sum_up = quant_grads(*slopes_up, dot(rows_u, pre_grad, FIRST))
    dw_down, sum_down = quant_grads(*slopes_down, dot(hidden_b, rows_c, FIRST))
    root = math.sqrt(w_up.size * parts * qlimit)
    ds_up, ds_down = sum_up / root, sum_down / root
    sums = jnp.stack([is_mine * ds_up, is_mine * ds_down])
    for c in range(peers.bit_length() - 1):
        sums = sums + swap(sums, 1 << c)

    rows_a = jnp.concatenate(after(blocks_a, dw_up, dw_down), axis=0)
    own_pre_a = dot(rows_a, q_up)
    pre_a = rounded(part_sum(own_pre_a))
    hidden_a = (pre_a * jax.nn.sigmoid(pre_a)).astype(jnp.bfloat16)
    ready = [None] * CHUNKS
    for c in (CHUNKS - 1, *range(CHUNKS - 1)):
        low, high = spans[c]
        ready[c] = dot(hidden_a, q_down[:, low:high]).astype(jnp.bfloat16)
    ready[-1] = ahead(ready[-1])
    ready[0] = after(ready[0], blocks_back[-1])
    chunks = [exchange(split(rows)) for rows in ready]

    grad = dot(hot_b, back)
    x_wide = x_b.astype(jnp.float32)
    own_inner = jnp.sum(x_wide * grad, axis=1, keepdims=True)
    inner = token_sum(own_inner)
    pull = rms_b * rms_b * rms_b * inner / width
    grad_in = c_b.astype(jnp.float32) + (rms_b * grad - x_wide * pull)
    next_cot = in_columns([pass_on(grad_in.astype(jnp.bfloat16), -1)])

    passed = []
    for c, (x_c, gates_c, hots_c) in enumerate(sources):
        done_a = jnp.concatenate(chunks[c], axis=0)
        mixed = x_c.astype(jnp.float32)
        taken = jnp.split(dot(jnp.concatenate(hots_c, axis=0), done_a), top, axis=0)
        for j, rows in enumerate(taken):
            mixed = mixed + gates_c[:, j : j + 1] * rows
        mixed = mixed.astype(jnp.bfloat16)
        if c < CHUNKS - 1:
            passed.append(pass_on(mixed, 1))
        else:
            pieces = jnp.split(mixed, parts, axis=0)
            passed.append([swap(piece, k) if k else piece for k, piece in enumerate(pieces)])
    next_a = in_columns(passed)
    return (
        next_a[None],
        next_cot[None],
        dw_up[None],
        dw_down[None],
        sums[0][None],
        sums[1][None],
    )


def solution(mesh):
    tokens = P("pipe", "expert", None)
    columns = P("pipe", None, "expert")
    steps = P("pipe", None)
    return jax.shard_map(
        section,
        mesh=mesh,
        in_specs=(tokens,) * 8 + (columns, steps, steps),
        out_specs=(tokens, tokens, tokens, columns, steps, steps),
        check_vma=False,
    )
```
